32 devices in a mesh: dp: 4 (over y, core), mp: 8 (over z, x).
Axes of the slice: x: 2, y: 2, z: 4, core: 2. Of those that a mesh axis runs over, the one named last changes fastest.
Arguments:
- gradient: float32 [8192, 16384], P(('dp', 'mp')), may hold values from -2000 to 2000
- left_basis: float32 [8192, 1024], P(('dp', 'mp')), may hold values from -1 to 1, as said below
- left_values: float32 [8192], P(('dp', 'mp')), may hold values from 0.05 to 2
- right_candidates: float32 [4, 16384, 256], P('dp', 'mp'), may hold values from -1 to 1, as said below
- right_owner: int32 [64], P('mp'), may hold values from 0 to 3
- right_values: float32 [16384], P('mp'), may hold values from 0.05 to 2
Outputs:
- direction: float32 [8192, 16384], P(('dp', 'mp'))
The draws below stay inside these ranges and needn't reach their ends.
Inputs may be any that keep to these rules, and one draw needn't show every extreme that they name: Each block of 1024 rows of left_basis is an orthogonal 1024 x 1024 matrix. For every data group, each block of 256 rows of right_candidates is an orthogonal 256 x 256 matrix. right_owner[j] names the data group whose copy of column block j is current.
All inputs are finite; a program needn't handle non-finite values.
Results may differ from the reference program's by a relative error of at most 0.00011.
Values sent between devices are 32-bit elements; how exact they have to be, the bound alone decides.
A program may use at most 128 MiB of HBM per device.

```python
import math
import jax
import jax.numpy as jnp
from jax import lax

D = 8192
FW = 16384
BL = 1024
BR = 256
N_DP = 4


def orthogonal_blocks(key, number, size):
    normals = jax.random.normal(key, (number, size, size), jnp.float32)
    factor, upper = jnp.linalg.qr(normals)
    return factor


def draw_gradient(key, part):
    key_values, key_rows, key_cols = jax.random.split(jax.random.fold_in(key, 7), 3)
    ramp = jnp.arange(D, dtype=jnp.float32) / (D - 1)
    row_scale = jnp.exp(jax.random.uniform(key_rows, (D,), jnp.float32, 0.0, math.log(10.0)))
    col_scale = jnp.exp(jax.random.uniform(key_cols, (FW,), jnp.float32, 0.0, math.log(10.0)))
    values = jnp.clip(jax.random.normal(key_values, (D, FW), jnp.float32), -6.0, 6.0)
    row_scale = row_scale * jnp.exp(math.log(3.0) * 0.5 * ramp)
    return values * row_scale[:, None] * col_scale[None, :]


def draw_left_basis(key, part):
    blocks = orthogonal_blocks(jax.random.fold_in(key, 11), D // BL, BL)
    return blocks.reshape(D, BL)


def draw_right_candidates(key, part):
    blocks = orthogonal_blocks(jax.random.fold_in(key, 13), N_DP * (FW // BR), BR)
    return blocks.reshape(N_DP, FW, BR)


def place_ends(values, rng, least, top_value):
    extent = values.shape
    place = [jax.random.randint(jax.random.fold_in(rng, axis), (), 0, extent[axis]) for axis in range(len(extent))]
    values = values.at[tuple(place)].set(least)
    longest = extent.index(max(extent))
    place[longest] = (place[longest] + 1) % extent[longest]
    return values.at[tuple(place)].set(top_value)


def shard_levels(rng, dims, shards, least, high):
    gain, own = 1.0, jax.random.fold_in(rng, 6)
    for dim, parts in shards:
        steps = jnp.exp(jax.random.uniform(jax.random.fold_in(own, dim), (parts,), jnp.float32, least / len(shards), high / len(shards)))
        gain = gain * jnp.repeat(steps, dims[dim] // parts).reshape([-1 if axis == dim else 1 for axis in range(len(dims))])
    return gain


def setup_inputs(seed: int = 0) -> dict:
    keys = jax.random.split(jax.random.key(seed), 7)
    return {
        "gradient": draw_gradient(jax.random.fold_in(keys[6], 71), 0),
        "left_basis": draw_left_basis(jax.random.fold_in(keys[6], 71), 0),
        "left_values": jnp.clip(jnp.exp(math.log(2.0) - 3.6888794 * jax.random.uniform(keys[2], (D,), jnp.float32) ** shard_levels(keys[2], (D,), ((0, 32),), -0.2, 0.2)), 0.05, 2.0),
        "right_candidates": draw_right_candidates(jax.random.fold_in(keys[6], 71), 0),
        "right_owner": place_ends(jax.random.randint(keys[4], (FW // BR,), 0, N_DP), jax.random.fold_in(keys[4], 1), 0, N_DP - 1).astype(jnp.int32),
        "right_values": jnp.clip(jnp.exp(math.log(2.0) - 3.6888794 * jax.random.uniform(keys[5], (FW,), jnp.float32) ** shard_levels(keys[5], (FW,), ((0, 8),), -0.2, 0.2)), 0.05, 2.0),
    }


damping = 0.01
epsilon = 1e-06
highest = lax.Precision.HIGHEST

def reference(gradient, left_basis, left_values, right_candidates, right_owner, right_values):
    left_count = D // BL
    right_count = FW // BR
    left_cubes = left_basis.reshape(left_count, BL, BL)
    stacked = right_candidates.reshape(N_DP, right_count, BR, BR)
    right_bases = stacked[right_owner, jnp.arange(right_count, dtype=jnp.int32)]
    right_lam = right_values.reshape(right_count, BR)
    grad_slabs = gradient.reshape(left_count, BL, right_count, BR)
    lam_slabs = left_values.reshape(left_count, BL)

    def one_block(inputs):
        left_block, grad_slab, lam_rows = inputs
        rotated = jnp.einsum('ra,rjc->ajc', left_block, grad_slab, precision=highest)
        rotated = jnp.einsum('ajc,jcd->ajd', rotated, right_bases, precision=highest)
        scaled = rotated / (lam_rows[:, None, None] + right_lam[None] + damping)
        restored = jnp.einsum('ajd,jcd->ajc', scaled, right_bases, precision=highest)
        return jnp.einsum('ra,ajc->rjc', left_block, restored, precision=highest)
    result = lax.map(one_block, (left_cubes, grad_slabs, lam_slabs)).reshape(D, FW)
    mean_square = jnp.sum(result * result) / (D * FW)
    return result * lax.rsqrt(mean_square + epsilon)
```

```python
import functools

import jax
import jax.numpy as jnp
from jax import lax
from jax.experimental import pallas as pl
from jax.experimental.pallas import tpu as pltpu
from jax.sharding import PartitionSpec as P

BL = 1024
BR = 256
WINDOW = 5
HOOK = 3

damping = 0.01
epsilon = 1e-06

MESH = pl.DeviceIdType.MESH
F32 = jnp.float32
BF16 = jnp.bfloat16


def flip(index, mask):
    bit = 1
    while bit <= mask:
        if mask & bit:
            index = index + bit - 2 * bit * ((index // bit) % 2)
        bit *= 2
    return index


def halves(value):
    head = value.astype(BF16)
    return head, (value - head.astype(F32)).astype(BF16)


def product(a_head, a_tail, b_head, b_tail, dims):
    def dot(a, b):
        return lax.dot_general(a, b, (dims, ((), ())), preferred_element_type=F32)

    return dot(a_head, b_head) + (dot(a_head, b_tail) + dot(a_tail, b_head))


NN = ((1,), (0,))
NT = ((1,), (1,))


def kernel(
    n_dp, n_mp, rows, members, families, span, blocks,
    grad, left, lvals, cand, owner, rvals,
    out, total,
    inbuf, lfull, lh, ll, lth, ltl, lev, lvbuf, lam, chosen, parts, right, sqbuf, acc,
    in_send, in_recv, out_send, out_recv, own_in, own_out,
    l_send, l_recv, lv_send, lv_recv, rs_send, rs_recv, ag_send, ag_recv, sw_send, sw_recv,
    lam_send, lam_recv, sq_send, sq_recv, loc,
):
    dp = lax.axis_index("dp")
    mp = lax.axis_index("mp")
    seat = mp % members
    family = mp // members
    part_rows = span // n_dp
    count = families * blocks

    def member(k):
        return family * members + flip(seat, k)

    def cousin(s, sign):
        return ((family + sign * s + families) % families) * members + seat

    def remote(src, dst, send, recv, d, m):
        return pltpu.make_async_remote_copy(
            src_ref=src, dst_ref=dst, send_sem=send, recv_sem=recv,
            device_id=(d, m), device_id_type=MESH,
        )

    cand_copy = pltpu.make_async_copy(cand.at[0], chosen, loc.at[0])
    cand_copy.start()
    left_copy = pltpu.make_async_copy(
        left, lfull.at[pl.ds(pl.multiple_of(seat * rows, rows), rows), :], loc.at[1]
    )
    left_copy.start()
    lam_copy = pltpu.make_async_copy(rvals, lam.at[0], loc.at[2])
    lam_copy.start()
    lv_copy = pltpu.make_async_copy(lvals, lvbuf.at[seat], loc.at[3])
    lv_copy.start()

    def column(c, who):
        s, j = c // blocks, c % blocks
        col = (((family + s) % families) * members + who) * span + j * BR
        return pl.ds(pl.multiple_of(col, BR), BR)

    def row_part(who):
        return pl.ds(pl.multiple_of(who * rows, rows), rows)

    def own_in_copy(c):
        return pltpu.make_async_copy(
            grad.at[:, column(c, seat)], inbuf.at[c, row_part(seat), :], own_in.at[c]
        )

    def in_copy(c, k):
        return remote(
            grad.at[:, column(c, flip(seat, k))], inbuf.at[c, row_part(seat), :],
            in_send.at[c, k - 1], in_recv.at[c, k - 1], dp, member(k),
        )

    def in_arrival(c, k):
        who = flip(seat, k)
        return remote(
            grad.at[:, column(c, seat)], inbuf.at[c, row_part(who), :],
            in_send.at[c, k - 1], in_recv.at[c, k - 1], dp, member(k),
        )

    def out_copy(c, k):
        who = flip(seat, k)
        return remote(
            inbuf.at[c, row_part(who), :], out.at[:, column(c, seat)],
            out_send.at[c, k - 1], out_recv.at[c, k - 1], dp, member(k),
        )

    def out_arrival(c, k):
        who = flip(seat, k)
        return remote(
            inbuf.at[c, row_part(who), :], out.at[:, column(c, who)],
            out_send.at[c, k - 1], out_recv.at[c, k - 1], dp, member(k),
        )

    def own_out_copy(c):
        return pltpu.make_async_copy(
            inbuf.at[c, row_part(seat), :], out.at[:, column(c, seat)], own_out.at[c]
        )

    partners = [(0, k) for k in range(1, members)]
    barrier = pltpu.get_barrier_semaphore()
    greeted = 0
    for k in range(1, members):
        pl.semaphore_signal(barrier, inc=1, device_id=(dp, member(k)), device_id_type=MESH)
        greeted += 1
    for s in range(1, families):
        pl.semaphore_signal(barrier, inc=1, device_id=(dp, cousin(s, 1)), device_id_type=MESH)
        greeted += 1
    for e in range(1, n_dp):
        pl.semaphore_signal(barrier, inc=1, device_id=(flip(dp, e), mp), device_id_type=MESH)
        greeted += 1
    pl.semaphore_wait(barrier, greeted)

    bits = []
    bit = 1
    while bit < members:
        bits.append(bit)
        bit *= 2
    orders = (bits, bits[::-1])
    half_rows = rows // 2

    def l_rows(who, half):
        start = who * rows + half * half_rows
        return pl.ds(pl.multiple_of(start, half_rows), half_rows)

    def l_round(half, r):
        order = orders[half]
        pieces = []
        for i in range(2 ** r):
            mask = 0
            for b in range(r):
                if i & (1 << b):
                    mask |= order[b]
            pieces.append((2 ** r - 1 + i, mask))
        return order[r], pieces

    def l_copy(half, bit, slot, mask):
        who = flip(seat, mask)
        where = l_rows(who, half)
        if mask:
            src = lfull.at[where, :]
        else:
            src = left.at[pl.ds(half * half_rows, half_rows), :]
        return remote(
            src, lfull.at[where, :], l_send.at[half, slot], l_recv.at[half, slot],
            dp, member(bit),
        )

    def l_arrival(half, bit, slot, mask):
        where = l_rows(flip(seat, mask ^ bit), half)
        return remote(
            lfull.at[where, :], lfull.at[where, :], l_send.at[half, slot], l_recv.at[half, slot],
            dp, member(bit),
        )

    def l_start(r):
        for half in range(2):
            bit, pieces = l_round(half, r)
            for slot, mask in pieces:
                l_copy(half, bit, slot, mask).start()

    def l_wait(r):
        for half in range(2):
            bit, pieces = l_round(half, r)
            for slot, mask in pieces:
                l_arrival(half, bit, slot, mask).wait_recv()

    l_start(0)
    for k in range(1, members):
        remote(
            lvals, lvbuf.at[seat], lv_send.at[k - 1], lv_recv.at[k - 1], dp, member(k)
        ).start()
    for s in range(1, families):
        remote(
            rvals, lam.at[s], lam_send.at[s - 1], lam_recv.at[s - 1], dp, cousin(s, -1)
        ).start()

    cand_copy.wait()

    def keep(b, carry):
        here = pl.ds(pl.multiple_of(b * BR, BR), BR)
        chosen[here, :] = jnp.where(owner[b] == dp, chosen[here, :], 0.0)
        return carry

    lax.fori_loop(0, blocks, keep, 0)

    def part(d):
        return pl.ds(pl.multiple_of(d * part_rows, part_rows), part_rows)

    def rs_copy(e):
        other = flip(dp, e)
        return remote(
            chosen.at[part(other), :], parts.at[e - 1],
            rs_send.at[e - 1], rs_recv.at[e - 1], other, mp,
        )

    def ag_copy(s, e):
        other = flip(dp, e)
        return remote(
            right.at[s, part(dp), :], right.at[s, part(dp), :],
            ag_send.at[s, e - 1], ag_recv.at[s, e - 1], other, mp,
        )

    def ag_arrival(s, e):
        other = flip(dp, e)
        return remote(
            right.at[s, part(other), :], right.at[s, part(other), :],
            ag_send.at[s, e - 1], ag_recv.at[s, e - 1], other, mp,
        )

    def sw_copy(s):
        return remote(
            right.at[0, part(dp), :], right.at[s, part(dp), :],
            sw_send.at[s - 1], sw_recv.at[s - 1], dp, cousin(s, -1),
        )

    for e in range(1, n_dp):
        rs_copy(e).start()

    for r in range(len(bits)):
        if r + 1 < len(bits):
            l_wait(r)
            l_start(r + 1)

    first = min(WINDOW, count)

    def begin(c, carry):
        own_in_copy(c).start()
        for k in range(1, members):
            in_copy(c, k).start()
        return carry

    lax.fori_loop(0, first, begin, 0)

    for e in range(1, n_dp):
        rs_copy(e).wait_recv()
    share = chosen[part(dp), :]
    for e in range(1, n_dp):
        share = share + parts[e - 1]
    right[0, part(dp), :] = share
    for s in range(1, families):
        sw_copy(s).start()
    for e in range(1, n_dp):
        ag_copy(0, e).start()

    lv_copy.wait()
    for k in range(1, members):
        remote(
            lvals, lvbuf.at[flip(seat, k)], lv_send.at[k - 1], lv_recv.at[k - 1], dp, member(k)
        ).wait_recv()

    def spread(m, carry):
        row = jnp.broadcast_to(lvbuf[m], (128, rows))
        lev[row_part(m), :] = row.T + damping
        return carry

    lax.fori_loop(0, members, spread, 0)
    lam_copy.wait()
    for s in range(1, families):
        remote(
            rvals, lam.at[s], lam_send.at[s - 1], lam_recv.at[s - 1], dp, cousin(s, -1)
        ).wait_recv()

    left_copy.wait()
    if bits:
        l_wait(len(bits) - 1)

    def prepare(i, carry):
        here = pl.ds(pl.multiple_of(i * BR, BR), BR)
        head, tail = halves(lfull[here, :])
        lh[here, :] = head
        ll[here, :] = tail
        for j in range(BL // BR):
            cols = slice(j * BR, (j + 1) * BR)
            head, tail = halves(lfull[here, cols].T)
            lth[cols, here] = head
            ltl[cols, here] = tail
        return carry

    lax.fori_loop(0, BL // BR, prepare, 0)
    acc[...] = jnp.zeros_like(acc)

    for e in range(1, n_dp):
        ag_arrival(0, e).wait_recv()

    def step(c, carry):
        @pl.when(c + WINDOW < count)
        def _():
            begin(c + WINDOW, 0)

        for s in range(1, families):
            @pl.when(c == min(s * blocks - 1, HOOK + s - 1))
            def _():
                sw_copy(s).wait_recv()
                for e in range(1, n_dp):
                    ag_copy(s, e).start()

            @pl.when(c == s * blocks)
            def _():
                for e in range(1, n_dp):
                    ag_arrival(s, e).wait_recv()

        own_in_copy(c).wait()
        for k in range(1, members):
            in_arrival(c, k).wait_recv()
        s, j = c // blocks, c % blocks
        here = pl.ds(pl.multiple_of(j * BR, BR), BR)
        basis_head, basis_tail = halves(right[s, here, :])
        head, tail = halves(inbuf[c])
        rotated = product(lth[...], ltl[...], head, tail, NN)
        head, tail = halves(rotated)
        turned = product(head, tail, basis_head, basis_tail, NN)
        levels = jnp.concatenate([lev[...]] * (BR // 128), axis=1)
        scaled = turned / (levels + lam[s, :, here])
        acc[...] += jnp.sum((scaled * scaled).reshape(BL // 8, 8, BR), axis=0)
        head, tail = halves(scaled)
        restored = product(head, tail, basis_head, basis_tail, NT)
        head, tail = halves(restored)
        inbuf[c] = product(lh[...], ll[...], head, tail, NN)
        for k in range(1, members):
            out_copy(c, k).start()
        own_out_copy(c).start()
        return carry

    lax.fori_loop(0, count, step, 0)

    mine = acc[:, :128]
    for j in range(1, BR // 128):
        mine = mine + acc[:, j * 128 : (j + 1) * 128]
    turn = 0
    steps = []
    bit = 1
    while bit < n_dp:
        steps.append((flip(dp, bit), mp))
        bit *= 2
    bit = 1
    while bit < members:
        steps.append((dp, member(bit)))
        bit *= 2
    for d, m in steps:
        sqbuf[2 * turn] = mine
        copy = remote(
            sqbuf.at[2 * turn], sqbuf.at[2 * turn + 1], sq_send.at[turn], sq_recv.at[turn], d, m
        )
        copy.start()
        copy.wait_recv()
        mine = mine + sqbuf[2 * turn + 1]
        turn += 1
    sqbuf[2 * turn] = mine
    whole = mine
    for s in range(1, families):
        copy = remote(
            sqbuf.at[2 * turn], sqbuf.at[2 * turn + s],
            sq_send.at[turn + s - 1], sq_recv.at[turn + s - 1], dp, cousin(s, 1),
        )
        copy.start()
    for s in range(1, families):
        remote(
            sqbuf.at[2 * turn], sqbuf.at[2 * turn + s],
            sq_send.at[turn + s - 1], sq_recv.at[turn + s - 1], dp, cousin(s, 1),
        ).wait_recv()
        whole = whole + sqbuf[2 * turn + s]
    total[...] = whole

    def finish(c, carry):
        own_out_copy(c).wait()
        for k in range(1, members):
            in_copy(c, k).wait_send()
            out_copy(c, k).wait_send()
            out_arrival(c, k).wait_recv()
        return carry

    for r in range(len(bits)):
        for half in range(2):
            bit, pieces = l_round(half, r)
            for slot, mask in pieces:
                l_copy(half, bit, slot, mask).wait_send()
    for k in range(1, members):
        remote(
            lvals, lvbuf.at[seat], lv_send.at[k - 1], lv_recv.at[k - 1], dp, member(k)
        ).wait_send()
    for s in range(1, families):
        remote(
            rvals, lam.at[s], lam_send.at[s - 1], lam_recv.at[s - 1], dp, cousin(s, -1)
        ).wait_send()
        sw_copy(s).wait_send()
        remote(
            sqbuf.at[2 * turn], sqbuf.at[2 * turn + s],
            sq_send.at[turn + s - 1], sq_recv.at[turn + s - 1], dp, cousin(s, 1),
        ).wait_send()
    for e in range(1, n_dp):
        rs_copy(e).wait_send()
        for s in range(families):
            ag_copy(s, e).wait_send()
    for i, (d, m) in enumerate(steps):
        remote(
            sqbuf.at[2 * i], sqbuf.at[2 * i + 1], sq_send.at[i], sq_recv.at[i], d, m
        ).wait_send()
    lax.fori_loop(0, count, finish, 0)


def solution(mesh):
    n_dp, n_mp = mesh.shape["dp"], mesh.shape["mp"]

    def on_device(gradient, left_basis, left_values, candidates, owner, right_values):
        rows, total_cols = gradient.shape
        members = BL // rows
        families = n_mp // members
        assert members * rows == BL and members * families == n_mp
        span = total_cols // n_mp
        blocks = span // BR
        count = families * blocks
        rounds = (n_dp - 1).bit_length() + (members - 1).bit_length()
        dma = pltpu.SemaphoreType.DMA
        many = max(members - 1, 1)
        others = max(families - 1, 1)
        anywhere = pl.BlockSpec(memory_space=pl.ANY)
        flops = 3 * 2 * BL * count * BR * (2 * BL + 2 * BR)
        raw, total = pl.pallas_call(
            functools.partial(kernel, n_dp, n_mp, rows, members, families, span, blocks),
            out_shape=(
                jax.ShapeDtypeStruct((rows, total_cols), F32),
                jax.ShapeDtypeStruct((8, 128), F32),
            ),
            in_specs=[
                anywhere, anywhere, anywhere, anywhere,
                pl.BlockSpec(memory_space=pltpu.SMEM), anywhere,
            ],
            out_specs=(anywhere, pl.BlockSpec(memory_space=pltpu.VMEM)),
            scratch_shapes=[
                pltpu.VMEM((count, BL, BR), F32),
                pltpu.VMEM((BL, BL), F32),
                pltpu.VMEM((BL, BL), BF16),
                pltpu.VMEM((BL, BL), BF16),
                pltpu.VMEM((BL, BL), BF16),
                pltpu.VMEM((BL, BL), BF16),
                pltpu.VMEM((BL, 128), F32),
                pltpu.VMEM((members, 1, rows), F32),
                pltpu.VMEM((families, 1, span), F32),
                pltpu.VMEM((span, BR), F32),
                pltpu.VMEM((n_dp - 1, span // n_dp, BR), F32),
                pltpu.VMEM((families, span, BR), F32),
                pltpu.VMEM((2 * rounds + families, 8, 128), F32),
                pltpu.VMEM((8, BR), F32),
                dma((count, many)), dma((count, many)), dma((count, many)), dma((count, many)),
                dma((count,)), dma((count,)),
                dma((2, many)), dma((2, many)), dma((many,)), dma((many,)),
                dma((n_dp - 1,)), dma((n_dp - 1,)),
                dma((families, n_dp - 1)), dma((families, n_dp - 1)),
                dma((others,)), dma((others,)), dma((others,)), dma((others,)),
                dma((rounds + others,)), dma((rounds + others,)),
                dma((4,)),
            ],
            compiler_params=pltpu.CompilerParams(
                collective_id=0, has_side_effects=True, vmem_limit_bytes=60 * 2**20
            ),
            cost_estimate=pl.CostEstimate(
                flops=flops, bytes_accessed=4 * rows * total_cols * 4, transcendentals=0
            ),
        )(
            gradient, left_basis, left_values.reshape(1, rows), candidates, owner,
            right_values.reshape(1, span),
        )
        mean_square = jnp.sum(total) / (rows * n_dp * n_mp * total_cols)
        return raw * lax.rsqrt(mean_square + epsilon)

    in_specs = (
        P(("dp", "mp"), None),
        P(("dp", "mp"), None),
        P(("dp", "mp")),
        P("dp", "mp", None),
        P("mp"),
        P("mp"),
    )
    return jax.shard_map(
        on_device, mesh=mesh, in_specs=in_specs, out_specs=P(("dp", "mp"), None), check_vma=False
    )
```

```python
import functools

import jax
import jax.numpy as jnp
from jax import lax
from jax.experimental import pallas as pl
from jax.experimental.pallas import tpu as pltpu
from jax.sharding import PartitionSpec as P

BL = 1024
BR = 256
AHEAD = 4
EARLY = 2
HOOK = 2
VMEM_MIB = 44

damping = 0.01
epsilon = 1e-06

MESH = pl.DeviceIdType.MESH
F32 = jnp.float32
BF16 = jnp.bfloat16


def flip(index, mask):
    bit = 1
    while bit <= mask:
        if mask & bit:
            index = index + bit - 2 * bit * ((index // bit) % 2)
        bit *= 2
    return index


def halves(value):
    head = value.astype(BF16)
    return head, (value - head.astype(F32)).astype(BF16)


def product(a_head, a_tail, b_head, b_tail, dims):
    def dot(a, b):
        return lax.dot_general(a, b, (dims, ((), ())), preferred_element_type=F32)

    return dot(a_head, b_head) + (dot(a_head, b_tail) + dot(a_tail, b_head))


NN = ((1,), (0,))
NT = ((1,), (1,))


def kernel(
    n_dp, n_mp, rows, members, families, span, blocks,
    grad, left, lvals, cand, owner, rvals,
    out,
    inbuf, lfull, lh, ll, lth, ltl, lev, lvbuf, lam, chosen, parts, right, sqbuf, acc, facbuf,
    in_send, in_recv, out_send, out_recv, own_in,
    l_send, l_recv, lv_send, lv_recv, rs_send, rs_recv, ag_send, ag_recv, sw_send, sw_recv,
    lam_send, lam_recv, sq_send, sq_recv, loc,
):
    dp = lax.axis_index("dp")
    mp = lax.axis_index("mp")
    seat = mp % members
    family = mp // members
    part_rows = span // n_dp
    count = families * blocks

    def member(k):
        return family * members + flip(seat, k)

    def cousin(s, sign):
        return ((family + sign * s + families) % families) * members + seat

    def remote(src, dst, send, recv, d, m):
        return pltpu.make_async_remote_copy(
            src_ref=src, dst_ref=dst, send_sem=send, recv_sem=recv,
            device_id=(d, m), device_id_type=MESH,
        )

    cand_copy = pltpu.make_async_copy(cand.at[0], chosen, loc.at[0])
    cand_copy.start()
    left_copy = pltpu.make_async_copy(
        left, lfull.at[pl.ds(pl.multiple_of(seat * rows, rows), rows), :], loc.at[1]
    )
    left_copy.start()
    lam_copy = pltpu.make_async_copy(rvals, lam.at[0], loc.at[2])
    lam_copy.start()
    lv_copy = pltpu.make_async_copy(lvals, lvbuf.at[seat], loc.at[3])
    lv_copy.start()

    def column(c, who):
        s, j = c // blocks, c % blocks
        col = (((family + s) % families) * members + who) * span + j * BR
        return pl.ds(pl.multiple_of(col, BR), BR)

    def row_part(who):
        return pl.ds(pl.multiple_of(who * rows, rows), rows)

    def own_in_copy(c):
        return pltpu.make_async_copy(
            grad.at[:, column(c, seat)], inbuf.at[c, row_part(seat), :], own_in.at[c]
        )

    def in_copy(c, k):
        return remote(
            grad.at[:, column(c, flip(seat, k))], inbuf.at[c, row_part(seat), :],
            in_send.at[c, k - 1], in_recv.at[c, k - 1], dp, member(k),
        )

    def in_arrival(c, k):
        who = flip(seat, k)
        return remote(
            grad.at[:, column(c, seat)], inbuf.at[c, row_part(who), :],
            in_send.at[c, k - 1], in_recv.at[c, k - 1], dp, member(k),
        )

    def out_copy(c, k):
        who = flip(seat, k)
        return remote(
            inbuf.at[c, row_part(who), :], out.at[:, column(c, seat)],
            out_send.at[c, k - 1], out_recv.at[c, k - 1], dp, member(k),
        )

    def out_arrival(c, k):
        who = flip(seat, k)
        return remote(
            inbuf.at[c, row_part(who), :], out.at[:, column(c, who)],
            out_send.at[c, k - 1], out_recv.at[c, k - 1], dp, member(k),
        )

    def each_peer(action):
        @pl.when(dp % 2 == 0)
        def _():
            for k in range(1, members):
                action(k)

        @pl.when(dp % 2 == 1)
        def _():
            for k in range(members - 1, 0, -1):
                action(k)

    def give(c):
        each_peer(lambda k: out_copy(c, k).start())

    barrier = pltpu.get_barrier_semaphore()
    greeted = 0
    for k in range(1, members):
        pl.semaphore_signal(barrier, inc=1, device_id=(dp, member(k)), device_id_type=MESH)
        greeted += 1
    for s in range(1, families):
        pl.semaphore_signal(barrier, inc=1, device_id=(dp, cousin(s, 1)), device_id_type=MESH)
        greeted += 1
    for e in range(1, n_dp):
        pl.semaphore_signal(barrier, inc=1, device_id=(flip(dp, e), mp), device_id_type=MESH)
        greeted += 1
    pl.semaphore_wait(barrier, greeted)

    bits = []
    bit = 1
    while bit < members:
        bits.append(bit)
        bit *= 2
    orders = (bits, bits[::-1])
    cut = rows // 4
    l_parts = ((0, cut), (cut, rows - cut))

    def l_rows(who, half):
        first, size = l_parts[half]
        return pl.ds(pl.multiple_of(who * rows + first, cut), size)

    def l_round(half, r):
        order = orders[half]
        pieces = []
        for i in range(2 ** r):
            mask = 0
            for b in range(r):
                if i & (1 << b):
                    mask |= order[b]
            pieces.append((2 ** r - 1 + i, mask))
        return order[r], pieces

    def l_copy(half, bit, slot, mask):
        who = flip(seat, mask)
        where = l_rows(who, half)
        if mask:
            src = lfull.at[where, :]
        else:
            src = left.at[pl.ds(*l_parts[half]), :]
        return remote(
            src, lfull.at[where, :], l_send.at[half, slot], l_recv.at[half, slot],
            dp, member(bit),
        )

    def l_arrival(half, bit, slot, mask):
        where = l_rows(flip(seat, mask ^ bit), half)
        return remote(
            lfull.at[where, :], lfull.at[where, :], l_send.at[half, slot], l_recv.at[half, slot],
            dp, member(bit),
        )

    def l_start(r):
        for half in range(2):
            bit, pieces = l_round(half, r)
            for slot, mask in pieces:
                l_copy(half, bit, slot, mask).start()

    def l_wait(r):
        for half in range(2):
            bit, pieces = l_round(half, r)
            for slot, mask in pieces:
                l_arrival(half, bit, slot, mask).wait_recv()

    def begin(c, carry):
        own_in_copy(c).start()
        each_peer(lambda k: in_copy(c, k).start())
        return carry

    l_start(0)
    early = min(EARLY, count)
    first = min(AHEAD, count)
    lax.fori_loop(0, early, begin, 0)
    for k in range(1, members):
        remote(
            lvals, lvbuf.at[seat], lv_send.at[k - 1], lv_recv.at[k - 1], dp, member(k)
        ).start()
    for s in range(1, families):
        remote(
            rvals, lam.at[s], lam_send.at[s - 1], lam_recv.at[s - 1], dp, cousin(s, -1)
        ).start()

    cand_copy.wait()

    def keep(b, carry):
        here = pl.ds(pl.multiple_of(b * BR, BR), BR)
        chosen[here, :] = jnp.where(owner[b] == dp, chosen[here, :], 0.0)
        return carry

    lax.fori_loop(0, blocks, keep, 0)

    def part(d):
        return pl.ds(pl.multiple_of(d * part_rows, part_rows), part_rows)

    def rs_copy(e):
        other = flip(dp, e)
        return remote(
            chosen.at[part(other), :], parts.at[e - 1],
            rs_send.at[e - 1], rs_recv.at[e - 1], other, mp,
        )

    def ag_copy(s, e):
        other = flip(dp, e)
        return remote(
            right.at[s, part(dp), :], right.at[s, part(dp), :],
            ag_send.at[s, e - 1], ag_recv.at[s, e - 1], other, mp,
        )

    def ag_arrival(s, e):
        other = flip(dp, e)
        return remote(
            right.at[s, part(other), :], right.at[s, part(other), :],
            ag_send.at[s, e - 1], ag_recv.at[s, e - 1], other, mp,
        )

    def sw_copy(s):
        return remote(
            right.at[0, part(dp), :], right.at[s, part(dp), :],
            sw_send.at[s - 1], sw_recv.at[s - 1], dp, cousin(s, -1),
        )

    for e in range(1, n_dp):
        rs_copy(e).start()

    for r in range(len(bits)):
        if r + 1 < len(bits):
            l_wait(r)
            l_start(r + 1)

    for e in range(1, n_dp):
        rs_copy(e).wait_recv()
    share = chosen[part(dp), :]
    for e in range(1, n_dp):
        share = share + parts[e - 1]
    right[0, part(dp), :] = share
    for s in range(1, families):
        sw_copy(s).start()
    for e in range(1, n_dp):
        ag_copy(0, e).start()
    lax.fori_loop(early, first, begin, 0)

    lv_copy.wait()
    for k in range(1, members):
        remote(
            lvals, lvbuf.at[flip(seat, k)], lv_send.at[k - 1], lv_recv.at[k - 1], dp, member(k)
        ).wait_recv()

    def spread(m, carry):
        row = jnp.broadcast_to(lvbuf[m], (128, rows))
        lev[row_part(m), :] = row.T + damping
        return carry

    lax.fori_loop(0, members, spread, 0)
    lam_copy.wait()
    for s in range(1, families):
        remote(
            rvals, lam.at[s], lam_send.at[s - 1], lam_recv.at[s - 1], dp, cousin(s, -1)
        ).wait_recv()

    left_copy.wait()
    if bits:
        l_wait(len(bits) - 1)

    def prepare(i, carry):
        here = pl.ds(pl.multiple_of(i * BR, BR), BR)
        head, tail = halves(lfull[here, :])
        lh[here, :] = head
        ll[here, :] = tail
        for j in range(BL // BR):
            cols = slice(j * BR, (j + 1) * BR)
            head, tail = halves(lfull[here, cols].T)
            lth[cols, here] = head
            ltl[cols, here] = tail
        return carry

    lax.fori_loop(0, BL // BR, prepare, 0)
    acc[...] = jnp.zeros_like(acc)

    for e in range(1, n_dp):
        ag_arrival(0, e).wait_recv()

    def step(c, carry):
        @pl.when(c + first < count)
        def _():
            begin(c + first, 0)

        @pl.when(c + first >= count + 1)
        def _():
            give(c + first - count - 1)

        for s in range(1, families):
            @pl.when(c == min(s * blocks - 1, HOOK + s - 1))
            def _():
                sw_copy(s).wait_recv()
                for e in range(1, n_dp):
                    ag_copy(s, e).start()

            @pl.when(c == s * blocks)
            def _():
                for e in range(1, n_dp):
                    ag_arrival(s, e).wait_recv()

        own_in_copy(c).wait()
        for k in range(1, members):
            in_arrival(c, k).wait_recv()
        s, j = c // blocks, c % blocks
        here = pl.ds(pl.multiple_of(j * BR, BR), BR)
        basis_head, basis_tail = halves(right[s, here, :])
        head, tail = halves(inbuf[c])
        rotated = product(lth[...], ltl[...], head, tail, NN)
        head, tail = halves(rotated)
        turned = product(head, tail, basis_head, basis_tail, NN)
        levels = jnp.concatenate([lev[...]] * (BR // 128), axis=1)
        scaled = turned / (levels + lam[s, :, here])
        acc[...] += jnp.sum((scaled * scaled).reshape(BL // 8, 8, BR), axis=0)
        head, tail = halves(scaled)
        restored = product(head, tail, basis_head, basis_tail, NT)
        head, tail = halves(restored)
        inbuf[c] = product(lh[...], ll[...], head, tail, NN)
        return carry

    lax.fori_loop(0, count, step, 0)

    given = first - 1
    queue = list(range(given, count))

    def give_next(number):
        for _ in range(number):
            if queue:
                c = queue.pop(0)
                if c - given >= 0 and c >= first:
                    for k in range(1, members):
                        out_copy(c - first, k).wait_send()
                give(c)

    give_next(1)

    mine = acc[:, :128]
    for j in range(1, BR // 128):
        mine = mine + acc[:, j * 128 : (j + 1) * 128]
    turn = 0
    steps = []
    bit = 1
    while bit < n_dp:
        steps.append((flip(dp, bit), mp))
        bit *= 2
    bit = 1
    while bit < members:
        steps.append((dp, member(bit)))
        bit *= 2
    for d, m in steps:
        sqbuf[2 * turn] = mine
        copy = remote(
            sqbuf.at[2 * turn], sqbuf.at[2 * turn + 1], sq_send.at[turn], sq_recv.at[turn], d, m
        )
        copy.start()
        if turn >= (n_dp - 1).bit_length():
            give_next(3)
        copy.wait_recv()
        mine = mine + sqbuf[2 * turn + 1]
        turn += 1
    sqbuf[2 * turn] = mine
    whole = mine
    for s in range(1, families):
        copy = remote(
            sqbuf.at[2 * turn], sqbuf.at[2 * turn + s],
            sq_send.at[turn + s - 1], sq_recv.at[turn + s - 1], dp, cousin(s, 1),
        )
        copy.start()
    give_next(3)
    for s in range(1, families):
        remote(
            sqbuf.at[2 * turn], sqbuf.at[2 * turn + s],
            sq_send.at[turn + s - 1], sq_recv.at[turn + s - 1], dp, cousin(s, 1),
        ).wait_recv()
        whole = whole + sqbuf[2 * turn + s]
    mean_square = jnp.sum(whole, keepdims=True) / (rows * n_dp * n_mp * span * n_mp)
    facbuf[...] = jnp.broadcast_to(lax.rsqrt(mean_square + epsilon), facbuf.shape)
    give_next(count)

    def finish(c, carry):
        factor = facbuf[0:1, :]
        out[:, column(c, seat)] = inbuf[c, row_part(seat), :] * factor
        for k in range(1, members):
            in_copy(c, k).wait_send()
            out_arrival(c, k).wait_recv()
            there = column(c, flip(seat, k))
            out[:, there] = out[:, there] * factor

        @pl.when(c >= count - first)
        def _():
            for k in range(1, members):
                out_copy(c, k).wait_send()

        return carry

    for r in range(len(bits)):
        for half in range(2):
            bit, pieces = l_round(half, r)
            for slot, mask in pieces:
                l_copy(half, bit, slot, mask).wait_send()
    for k in range(1, members):
        remote(
            lvals, lvbuf.at[seat], lv_send.at[k - 1], lv_recv.at[k - 1], dp, member(k)
        ).wait_send()
    for s in range(1, families):
        remote(
            rvals, lam.at[s], lam_send.at[s - 1], lam_recv.at[s - 1], dp, cousin(s, -1)
        ).wait_send()
        sw_copy(s).wait_send()
        remote(
            sqbuf.at[2 * turn], sqbuf.at[2 * turn + s],
            sq_send.at[turn + s - 1], sq_recv.at[turn + s - 1], dp, cousin(s, 1),
        ).wait_send()
    for e in range(1, n_dp):
        rs_copy(e).wait_send()
        for s in range(families):
            ag_copy(s, e).wait_send()
    for i, (d, m) in enumerate(steps):
        remote(
            sqbuf.at[2 * i], sqbuf.at[2 * i + 1], sq_send.at[i], sq_recv.at[i], d, m
        ).wait_send()
    lax.fori_loop(0, count, finish, 0)


def solution(mesh):
    n_dp, n_mp = mesh.shape["dp"], mesh.shape["mp"]

    def on_device(gradient, left_basis, left_values, candidates, owner, right_values):
        rows, total_cols = gradient.shape
        members = BL // rows
        families = n_mp // members
        assert members * rows == BL and members * families == n_mp
        span = total_cols // n_mp
        blocks = span // BR
        count = families * blocks
        rounds = (n_dp - 1).bit_length() + (members - 1).bit_length()
        dma = pltpu.SemaphoreType.DMA
        many = max(members - 1, 1)
        others = max(families - 1, 1)
        anywhere = pl.BlockSpec(memory_space=pl.ANY)
        flops = 3 * 2 * BL * count * BR * (2 * BL + 2 * BR)
        return pl.pallas_call(
            functools.partial(kernel, n_dp, n_mp, rows, members, families, span, blocks),
            out_shape=pltpu.VMEM((rows, total_cols), F32),
            in_specs=[
                anywhere, anywhere, anywhere, anywhere,
                pl.BlockSpec(memory_space=pltpu.SMEM), anywhere,
            ],
            out_specs=pl.BlockSpec(memory_space=pltpu.VMEM),
            scratch_shapes=[
                pltpu.VMEM((count, BL, BR), F32),
                pltpu.VMEM((BL, BL), F32),
                pltpu.VMEM((BL, BL), BF16),
                pltpu.VMEM((BL, BL), BF16),
                pltpu.VMEM((BL, BL), BF16),
                pltpu.VMEM((BL, BL), BF16),
                pltpu.VMEM((BL, 128), F32),
                pltpu.VMEM((members, 1, rows), F32),
                pltpu.VMEM((families, 1, span), F32),
                pltpu.VMEM((span, BR), F32),
                pltpu.VMEM((n_dp - 1, span // n_dp, BR), F32),
                pltpu.VMEM((families, span, BR), F32),
                pltpu.VMEM((2 * rounds + families, 8, 128), F32),
                pltpu.VMEM((8, BR), F32),
                pltpu.VMEM((8, BR), F32),
                dma((count, many)), dma((count, many)), dma((count, many)), dma((count, many)),
                dma((count,)),
                dma((2, many)), dma((2, many)), dma((many,)), dma((many,)),
                dma((n_dp - 1,)), dma((n_dp - 1,)),
                dma((families, n_dp - 1)), dma((families, n_dp - 1)),
                dma((others,)), dma((others,)), dma((others,)), dma((others,)),
                dma((rounds + others,)), dma((rounds + others,)),
                dma((4,)),
            ],
            compiler_params=pltpu.CompilerParams(
                collective_id=0, has_side_effects=True, vmem_limit_bytes=VMEM_MIB * 2**20
            ),
            cost_estimate=pl.CostEstimate(
                flops=flops, bytes_accessed=4 * rows * total_cols * 4, transcendentals=0
            ),
        )(
            gradient, left_basis, left_values.reshape(1, rows), candidates, owner,
            right_values.reshape(1, span),
        )

    in_specs = (
        P(("dp", "mp"), None),
        P(("dp", "mp"), None),
        P(("dp", "mp")),
        P("dp", "mp", None),
        P("mp"),
        P("mp"),
    )
    return jax.shard_map(
        on_device, mesh=mesh, in_specs=in_specs, out_specs=P(("dp", "mp"), None), check_vma=False
    )
```

```python
import functools

import jax
import jax.numpy as jnp
from jax import lax
from jax.experimental import pallas as pl
from jax.experimental.pallas import tpu as pltpu
from jax.sharding import PartitionSpec as P

BL = 1024
BR = 256
AHEAD = 8
EARLY = 4
TAIL = 4
HOOK = 2
VMEM_MIB = 44

damping = 0.01
epsilon = 1e-06

MESH = pl.DeviceIdType.MESH
F32 = jnp.float32
BF16 = jnp.bfloat16


def flip(index, mask):
    bit = 1
    while bit <= mask:
        if mask & bit:
            index = index + bit - 2 * bit * ((index // bit) % 2)
        bit *= 2
    return index


def halves(value):
    head = value.astype(BF16)
    return head, (value - head.astype(F32)).astype(BF16)


def product(a_head, a_tail, b_head, b_tail, dims):
    def dot(a, b):
        return lax.dot_general(a, b, (dims, ((), ())), preferred_element_type=F32)

    return dot(a_head, b_head) + (dot(a_head, b_tail) + dot(a_tail, b_head))


NN = ((1,), (0,))
NT = ((1,), (1,))


def kernel(
    n_dp, n_mp, rows, members, families, span, blocks,
    grad, left, lvals, cand, owner, rvals,
    out,
    inbuf, lfull, lh, ll, lth, ltl, lev, lvbuf, lam, chosen, parts, right, sqbuf, acc, facbuf,
    in_send, in_recv, out_send, out_recv, own_in,
    l_send, l_recv, lv_send, lv_recv, rs_send, rs_recv, ag_send, ag_recv, sw_send, sw_recv,
    lam_send, lam_recv, sq_send, sq_recv, loc,
):
    dp = lax.axis_index("dp")
    mp = lax.axis_index("mp")
    seat = mp % members
    family = mp // members
    part_rows = span // n_dp
    count = families * blocks

    def member(k):
        return family * members + flip(seat, k)

    def cousin(s, sign):
        return ((family + sign * s + families) % families) * members + seat

    def remote(src, dst, send, recv, d, m):
        return pltpu.make_async_remote_copy(
            src_ref=src, dst_ref=dst, send_sem=send, recv_sem=recv,
            device_id=(d, m), device_id_type=MESH,
        )

    cand_copy = pltpu.make_async_copy(cand.at[0], chosen, loc.at[0])
    cand_copy.start()
    left_copy = pltpu.make_async_copy(
        left, lfull.at[pl.ds(pl.multiple_of(seat * rows, rows), rows), :], loc.at[1]
    )
    left_copy.start()
    lam_copy = pltpu.make_async_copy(rvals, lam.at[0], loc.at[2])
    lam_copy.start()
    lv_copy = pltpu.make_async_copy(lvals, lvbuf.at[seat], loc.at[3])
    lv_copy.start()

    def column(c, who):
        s, j = c // blocks, c % blocks
        col = (((family + s) % families) * members + who) * span + j * BR
        return pl.ds(pl.multiple_of(col, BR), BR)

    def row_part(who):
        return pl.ds(pl.multiple_of(who * rows, rows), rows)

    def own_in_copy(c):
        return pltpu.make_async_copy(
            grad.at[:, column(c, seat)], inbuf.at[c, row_part(seat), :], own_in.at[c]
        )

    def in_copy(c, k):
        return remote(
            grad.at[:, column(c, flip(seat, k))], inbuf.at[c, row_part(seat), :],
            in_send.at[c, k - 1], in_recv.at[c, k - 1], dp, member(k),
        )

    def in_arrival(c, k):
        who = flip(seat, k)
        return remote(
            grad.at[:, column(c, seat)], inbuf.at[c, row_part(who), :],
            in_send.at[c, k - 1], in_recv.at[c, k - 1], dp, member(k),
        )

    def out_copy(c, k):
        who = flip(seat, k)
        return remote(
            inbuf.at[c, row_part(who), :], out.at[:, column(c, seat)],
            out_send.at[c, k - 1], out_recv.at[c, k - 1], dp, member(k),
        )

    def out_arrival(c, k):
        who = flip(seat, k)
        return remote(
            inbuf.at[c, row_part(who), :], out.at[:, column(c, who)],
            out_send.at[c, k - 1], out_recv.at[c, k - 1], dp, member(k),
        )

    def each_peer(action):
        @pl.when(dp % 2 == 0)
        def _():
            for k in range(1, members):
                action(k)

        @pl.when(dp % 2 == 1)
        def _():
            for k in range(members - 1, 0, -1):
                action(k)

    near = [k for k in range(1, members) if k & (k - 1) == 0]
    far = [k for k in range(1, members) if k & (k - 1)]

    def give(c):
        each_peer(lambda k: out_copy(c, k).start())

    barrier = pltpu.get_barrier_semaphore()
    greeted = 0
    for k in range(1, members):
        pl.semaphore_signal(barrier, inc=1, device_id=(dp, member(k)), device_id_type=MESH)
        greeted += 1
    for s in range(1, families):
        pl.semaphore_signal(barrier, inc=1, device_id=(dp, cousin(s, 1)), device_id_type=MESH)
        greeted += 1
    for e in range(1, n_dp):
        pl.semaphore_signal(barrier, inc=1, device_id=(flip(dp, e), mp), device_id_type=MESH)
        greeted += 1
    pl.semaphore_wait(barrier, greeted)

    bits = []
    bit = 1
    while bit < members:
        bits.append(bit)
        bit *= 2
    orders = (bits, bits[::-1])
    cut = rows // 4
    l_parts = ((0, cut), (cut, rows - cut))

    def l_rows(who, half):
        first, size = l_parts[half]
        return pl.ds(pl.multiple_of(who * rows + first, cut), size)

    def l_round(half, r):
        order = orders[half]
        pieces = []
        for i in range(2 ** r):
            mask = 0
            for b in range(r):
                if i & (1 << b):
                    mask |= order[b]
            pieces.append((2 ** r - 1 + i, mask))
        return order[r], pieces

    def l_copy(half, bit, slot, mask):
        who = flip(seat, mask)
        where = l_rows(who, half)
        if mask:
            src = lfull.at[where, :]
        else:
            src = left.at[pl.ds(*l_parts[half]), :]
        return remote(
            src, lfull.at[where, :], l_send.at[half, slot], l_recv.at[half, slot],
            dp, member(bit),
        )

    def l_arrival(half, bit, slot, mask):
        where = l_rows(flip(seat, mask ^ bit), half)
        return remote(
            lfull.at[where, :], lfull.at[where, :], l_send.at[half, slot], l_recv.at[half, slot],
            dp, member(bit),
        )

    def l_start(r):
        for half in range(2):
            bit, pieces = l_round(half, r)
            for slot, mask in pieces:
                l_copy(half, bit, slot, mask).start()

    def l_wait(r):
        for half in range(2):
            bit, pieces = l_round(half, r)
            for slot, mask in pieces:
                l_arrival(half, bit, slot, mask).wait_recv()

    def begin(c, carry):
        own_in_copy(c).start()
        each_peer(lambda k: in_copy(c, k).start())
        return carry

    def begin_near(c, carry):
        own_in_copy(c).start()
        for k in near:
            in_copy(c, k).start()
        return carry

    def begin_far(c, carry):
        for k in far:
            in_copy(c, k).start()
        return carry

    l_start(0)
    early = min(EARLY, count)
    first = min(AHEAD, count)
    lax.fori_loop(0, early, begin_near, 0)
    for k in range(1, members):
        remote(
            lvals, lvbuf.at[seat], lv_send.at[k - 1], lv_recv.at[k - 1], dp, member(k)
        ).start()
    for s in range(1, families):
        remote(
            rvals, lam.at[s], lam_send.at[s - 1], lam_recv.at[s - 1], dp, cousin(s, -1)
        ).start()

    cand_copy.wait()

    def keep(b, carry):
        here = pl.ds(pl.multiple_of(b * BR, BR), BR)
        chosen[here, :] = jnp.where(owner[b] == dp, chosen[here, :], 0.0)
        return carry

    lax.fori_loop(0, blocks, keep, 0)

    def part(d):
        return pl.ds(pl.multiple_of(d * part_rows, part_rows), part_rows)

    def rs_copy(e):
        other = flip(dp, e)
        return remote(
            chosen.at[part(other), :], parts.at[e - 1],
            rs_send.at[e - 1], rs_recv.at[e - 1], other, mp,
        )

    def ag_copy(s, e):
        other = flip(dp, e)
        return remote(
            right.at[s, part(dp), :], right.at[s, part(dp), :],
            ag_send.at[s, e - 1], ag_recv.at[s, e - 1], other, mp,
        )

    def ag_arrival(s, e):
        other = flip(dp, e)
        return remote(
            right.at[s, part(other), :], right.at[s, part(other), :],
            ag_send.at[s, e - 1], ag_recv.at[s, e - 1], other, mp,
        )

    def sw_copy(s):
        return remote(
            right.at[0, part(dp), :], right.at[s, part(dp), :],
            sw_send.at[s - 1], sw_recv.at[s - 1], dp, cousin(s, -1),
        )

    for e in range(1, n_dp):
        rs_copy(e).start()

    for r in range(len(bits)):
        if r + 1 < len(bits):
            l_wait(r)
            l_start(r + 1)
    lax.fori_loop(0, early, begin_far, 0)

    for e in range(1, n_dp):
        rs_copy(e).wait_recv()
    share = chosen[part(dp), :]
    for e in range(1, n_dp):
        share = share + parts[e - 1]
    right[0, part(dp), :] = share
    for s in range(1, families):
        sw_copy(s).start()
    for e in range(1, n_dp):
        ag_copy(0, e).start()
    lax.fori_loop(early, first, begin, 0)

    lv_copy.wait()
    for k in range(1, members):
        remote(
            lvals, lvbuf.at[flip(seat, k)], lv_send.at[k - 1], lv_recv.at[k - 1], dp, member(k)
        ).wait_recv()

    def spread(m, carry):
        row = jnp.broadcast_to(lvbuf[m], (128, rows))
        lev[row_part(m), :] = row.T + damping
        return carry

    lax.fori_loop(0, members, spread, 0)
    lam_copy.wait()
    for s in range(1, families):
        remote(
            rvals, lam.at[s], lam_send.at[s - 1], lam_recv.at[s - 1], dp, cousin(s, -1)
        ).wait_recv()

    left_copy.wait()
    if bits:
        l_wait(len(bits) - 1)

    def prepare(i, carry):
        here = pl.ds(pl.multiple_of(i * BR, BR), BR)
        head, tail = halves(lfull[here, :])
        lh[here, :] = head
        ll[here, :] = tail
        for j in range(BL // BR):
            cols = slice(j * BR, (j + 1) * BR)
            head, tail = halves(lfull[here, cols].T)
            lth[cols, here] = head
            ltl[cols, here] = tail
        return carry

    lax.fori_loop(0, BL // BR, prepare, 0)
    acc[...] = jnp.zeros_like(acc)

    for e in range(1, n_dp):
        ag_arrival(0, e).wait_recv()

    def step(c, carry):
        @pl.when(c + first < count)
        def _():
            begin(c + first, 0)

        @pl.when(c + first >= count + 1)
        def _():
            give(c + first - count - 1)

        for s in range(1, families):
            @pl.when(c == min(s * blocks - 1, HOOK + s - 1))
            def _():
                sw_copy(s).wait_recv()
                for e in range(1, n_dp):
                    ag_copy(s, e).start()

            @pl.when(c == s * blocks)
            def _():
                for e in range(1, n_dp):
                    ag_arrival(s, e).wait_recv()

        own_in_copy(c).wait()
        for k in range(1, members):
            in_arrival(c, k).wait_recv()
        s, j = c // blocks, c % blocks
        here = pl.ds(pl.multiple_of(j * BR, BR), BR)
        basis_head, basis_tail = halves(right[s, here, :])
        head, tail = halves(inbuf[c])
        rotated = product(lth[...], ltl[...], head, tail, NN)
        head, tail = halves(rotated)
        turned = product(head, tail, basis_head, basis_tail, NN)
        levels = jnp.concatenate([lev[...]] * (BR // 128), axis=1)
        scaled = turned / (levels + lam[s, :, here])
        acc[...] += jnp.sum((scaled * scaled).reshape(BL // 8, 8, BR), axis=0)
        head, tail = halves(scaled)
        restored = product(head, tail, basis_head, basis_tail, NT)
        head, tail = halves(restored)
        inbuf[c] = product(lh[...], ll[...], head, tail, NN)
        return carry

    lax.fori_loop(0, count, step, 0)

    given = first - 1
    queue = list(range(given, count))
    last = []

    def give_next(number):
        for _ in range(number):
            if queue:
                c = queue.pop(0)
                if c - given >= 0 and c >= first:
                    for k in range(1, members):
                        out_copy(c - first, k).wait_send()
                if c < count - TAIL:
                    give(c)
                    continue
                for k in far:
                    out_copy(c, k).start()
                last.append(c)
        if not queue:
            while last:
                c = last.pop(0)
                for k in near:
                    out_copy(c, k).start()

    give_next(1)

    mine = acc[:, :128]
    for j in range(1, BR // 128):
        mine = mine + acc[:, j * 128 : (j + 1) * 128]
    turn = 0
    steps = []
    bit = 1
    while bit < n_dp:
        steps.append((flip(dp, bit), mp))
        bit *= 2
    bit = 1
    while bit < members:
        steps.append((dp, member(bit)))
        bit *= 2
    for d, m in steps:
        sqbuf[2 * turn] = mine
        copy = remote(
            sqbuf.at[2 * turn], sqbuf.at[2 * turn + 1], sq_send.at[turn], sq_recv.at[turn], d, m
        )
        copy.start()
        if turn >= (n_dp - 1).bit_length():
            give_next(3)
        copy.wait_recv()
        mine = mine + sqbuf[2 * turn + 1]
        turn += 1
    sqbuf[2 * turn] = mine
    whole = mine
    for s in range(1, families):
        copy = remote(
            sqbuf.at[2 * turn], sqbuf.at[2 * turn + s],
            sq_send.at[turn + s - 1], sq_recv.at[turn + s - 1], dp, cousin(s, 1),
        )
        copy.start()
    give_next(3)
    for s in range(1, families):
        remote(
            sqbuf.at[2 * turn], sqbuf.at[2 * turn + s],
            sq_send.at[turn + s - 1], sq_recv.at[turn + s - 1], dp, cousin(s, 1),
        ).wait_recv()
        whole = whole + sqbuf[2 * turn + s]
    mean_square = jnp.sum(whole, keepdims=True) / (rows * n_dp * n_mp * span * n_mp)
    facbuf[...] = jnp.broadcast_to(lax.rsqrt(mean_square + epsilon), facbuf.shape)
    give_next(count)

    def finish(c, carry):
        factor = facbuf[0:1, :]
        out[:, column(c, seat)] = inbuf[c, row_part(seat), :] * factor
        for k in range(1, members):
            in_copy(c, k).wait_send()
            out_arrival(c, k).wait_recv()
            there = column(c, flip(seat, k))
            out[:, there] = out[:, there] * factor

        @pl.when(c >= count - first)
        def _():
            for k in range(1, members):
                out_copy(c, k).wait_send()

        return carry

    for r in range(len(bits)):
        for half in range(2):
            bit, pieces = l_round(half, r)
            for slot, mask in pieces:
                l_copy(half, bit, slot, mask).wait_send()
    for k in range(1, members):
        remote(
            lvals, lvbuf.at[seat], lv_send.at[k - 1], lv_recv.at[k - 1], dp, member(k)
        ).wait_send()
    for s in range(1, families):
        remote(
            rvals, lam.at[s], lam_send.at[s - 1], lam_recv.at[s - 1], dp, cousin(s, -1)
        ).wait_send()
        sw_copy(s).wait_send()
        remote(
            sqbuf.at[2 * turn], sqbuf.at[2 * turn + s],
            sq_send.at[turn + s - 1], sq_recv.at[turn + s - 1], dp, cousin(s, 1),
        ).wait_send()
    for e in range(1, n_dp):
        rs_copy(e).wait_send()
        for s in range(families):
            ag_copy(s, e).wait_send()
    for i, (d, m) in enumerate(steps):
        remote(
            sqbuf.at[2 * i], sqbuf.at[2 * i + 1], sq_send.at[i], sq_recv.at[i], d, m
        ).wait_send()
    lax.fori_loop(0, count, finish, 0)


def solution(mesh):
    n_dp, n_mp = mesh.shape["dp"], mesh.shape["mp"]

    def on_device(gradient, left_basis, left_values, candidates, owner, right_values):
        rows, total_cols = gradient.shape
        members = BL // rows
        families = n_mp // members
        assert members * rows == BL and members * families == n_mp
        span = total_cols // n_mp
        blocks = span // BR
        count = families * blocks
        rounds = (n_dp - 1).bit_length() + (members - 1).bit_length()
        dma = pltpu.SemaphoreType.DMA
        many = max(members - 1, 1)
        others = max(families - 1, 1)
        anywhere = pl.BlockSpec(memory_space=pl.ANY)
        flops = 3 * 2 * BL * count * BR * (2 * BL + 2 * BR)
        return pl.pallas_call(
            functools.partial(kernel, n_dp, n_mp, rows, members, families, span, blocks),
            out_shape=pltpu.VMEM((rows, total_cols), F32),
            in_specs=[
                anywhere, anywhere, anywhere, anywhere,
                pl.BlockSpec(memory_space=pltpu.SMEM), anywhere,
            ],
            out_specs=pl.BlockSpec(memory_space=pltpu.VMEM),
            scratch_shapes=[
                pltpu.VMEM((count, BL, BR), F32),
                pltpu.VMEM((BL, BL), F32),
                pltpu.VMEM((BL, BL), BF16),
                pltpu.VMEM((BL, BL), BF16),
                pltpu.VMEM((BL, BL), BF16),
                pltpu.VMEM((BL, BL), BF16),
                pltpu.VMEM((BL, 128), F32),
                pltpu.VMEM((members, 1, rows), F32),
                pltpu.VMEM((families, 1, span), F32),
                pltpu.VMEM((span, BR), F32),
                pltpu.VMEM((n_dp - 1, span // n_dp, BR), F32),
                pltpu.VMEM((families, span, BR), F32),
                pltpu.VMEM((2 * rounds + families, 8, 128), F32),
                pltpu.VMEM((8, BR), F32),
                pltpu.VMEM((8, BR), F32),
                dma((count, many)), dma((count, many)), dma((count, many)), dma((count, many)),
                dma((count,)),
                dma((2, many)), dma((2, many)), dma((many,)), dma((many,)),
                dma((n_dp - 1,)), dma((n_dp - 1,)),
                dma((families, n_dp - 1)), dma((families, n_dp - 1)),
                dma((others,)), dma((others,)), dma((others,)), dma((others,)),
                dma((rounds + others,)), dma((rounds + others,)),
                dma((4,)),
            ],
            compiler_params=pltpu.CompilerParams(
                collective_id=0, has_side_effects=True, vmem_limit_bytes=VMEM_MIB * 2**20
            ),
            cost_estimate=pl.CostEstimate(
                flops=flops, bytes_accessed=4 * rows * total_cols * 4, transcendentals=0
            ),
        )(
            gradient, left_basis, left_values.reshape(1, rows), candidates, owner,
            right_values.reshape(1, span),
        )

    in_specs = (
        P(("dp", "mp"), None),
        P(("dp", "mp"), None),
        P(("dp", "mp")),
        P("dp", "mp", None),
        P("mp"),
        P("mp"),
    )
    return jax.shard_map(
        on_device, mesh=mesh, in_specs=in_specs, out_specs=P(("dp", "mp"), None), check_vma=False
    )
```
